512 devices in a mesh: ctx: 64 (over z, y), head: 8 (over x, core).
Axes of the slice: x: 4, y: 4, z: 16, core: 2. Of those that a mesh axis runs over, the one named last changes fastest.
Arguments:
- tokens: bfloat16 [16384, 2048], P('ctx', 'head'), may hold values from -6 to 6
- qkv_weight: bfloat16 [2048, 3, 2048], P('ctx', None, 'head'), may hold values from -0.125 to 0.125
- out_gain: float32 [2048], P('head'), may hold values from 0.1 to 1.9
Outputs:
- attended: bfloat16 [16384, 2048], P('ctx', 'head')
The draws below stay inside these ranges and needn't reach their ends.
All inputs are finite; a program needn't handle non-finite values.
Results may differ from the reference program's by a relative error of at most 0.001.
Values may be sent and summed in bfloat16 or wider, within the bound.
No kernel may reach another device: no remote copies, remote signals or barrier semaphores. Data moves between devices by JAX's collectives and lax.ppermute only.
A program may use at most 64 MiB of HBM per device.

```python
import math
import jax
import jax.numpy as jnp
from jax import lax

D = 2048
HEADS = 16
HD = 128
TOK_DEV = 256
TOKENS = 16384


def shard_levels(rng, shape, cuts, low, high):
    loudness = 1.0
    for position, blocks in cuts:
        steps = jax.random.uniform(jax.random.fold_in(jax.random.fold_in(rng, 6), position), (blocks,), jnp.float32, low / len(cuts), high / len(cuts))
        loudness = loudness * jnp.repeat(jnp.exp(steps), shape[position] // blocks).reshape((-1,) + (1,) * (len(shape) - 1 - position))
    return loudness


def centred(own_key, shape, width, reach, pieces=(), kind=jnp.bfloat16):
    values = width * jax.random.normal(own_key, shape, jnp.float32)
    if pieces:
        values = values * shard_levels(own_key, shape, pieces, -0.22, 0.18)
    return jnp.clip(values, -reach, reach).astype(kind)


def setup_inputs(seed: int = 0) -> dict:
    seeds = jax.random.split(jax.random.key(seed), 4)
    tokens = centred(seeds[0], (TOKENS, D), 1.0, 6.0, ((0, 64), (1, 8)))
    qkv_weight = centred(seeds[1], (D, 3, HEADS * HD), D ** -0.5, 0.125, ((0, 64), (2, 8)))
    out_gain = jnp.clip(1.0 + 0.18 * jax.random.normal(seeds[2], (HEADS * HD,), jnp.float32), 0.1, 1.9)
    return dict(tokens=tokens, qkv_weight=qkv_weight, out_gain=out_gain)


epsilon = 1e-06
highest = lax.Precision.HIGHEST

def block_terms(queries, key_rows, val_rows, prior_s, prior_m):
    rows_here = queries.shape[0]
    row_ids = lax.broadcasted_iota(jnp.int32, (rows_here, rows_here), 0)
    col_ids = lax.broadcasted_iota(jnp.int32, (rows_here, rows_here), 1)
    causal = row_ids >= col_ids
    strict = row_ids < col_ids
    scores = jnp.einsum('thd,shd->hts', queries, key_rows, precision=highest)
    lower_part = jnp.where(causal, scores, 0.0)
    pair_term = jnp.einsum('hti,hji->htj', lower_part, lower_part, precision=highest)
    query_state = jnp.einsum('thd,hde->the', queries, prior_s, precision=highest)
    cross_term = jnp.einsum('the,she->hts', query_state, queries, precision=highest)
    mixing = jnp.where(causal, pair_term + cross_term, 0.0)
    raw_out = jnp.einsum('hts,she->the', mixing, val_rows, precision=highest)
    raw_out = raw_out + jnp.einsum('thd,hde->the', queries, prior_m, precision=highest)
    local_s = jnp.einsum('thd,the->hde', key_rows, key_rows, precision=highest)
    local_c = jnp.einsum('thd,the->hde', queries, val_rows, precision=highest)
    upper_part = jnp.where(strict, scores, 0.0)
    weighted = jnp.einsum('hji,jhe->ihe', upper_part, val_rows, precision=highest)
    local_g = jnp.einsum('ihd,ihe->hde', key_rows, weighted, precision=highest)
    return (raw_out, local_s, local_c, local_g)

def reference(tokens, qkv_weight, out_gain):
    block_len = math.gcd(TOK_DEV, 128)
    blocks = TOKENS // block_len
    flat_weight = qkv_weight.reshape(D, 3 * HEADS * HD)
    token_blocks = tokens.reshape(blocks, block_len, D)

    def step(carry, token_block):
        prior_s, prior_c, prior_g = carry
        projected = jnp.dot(token_block, flat_weight, preferred_element_type=jnp.float32)
        projected = projected.reshape(block_len, 3, HEADS, HD)
        queries = projected[:, 0]
        key_rows = projected[:, 1]
        val_rows = projected[:, 2]
        prior_m = jnp.einsum('hij,hjk->hik', prior_s, prior_c, precision=highest) - prior_g
        raw_out, local_s, local_c, local_g = block_terms(queries, key_rows, val_rows, prior_s, prior_m)
        next_g = prior_g + local_g + jnp.einsum('hij,hjk->hik', local_s, prior_c, precision=highest)
        return ((prior_s + local_s, prior_c + local_c, next_g), raw_out)
    zeros_state = jnp.zeros((HEADS, HD, HD), jnp.float32)
    carry, raw_all = lax.scan(step, (zeros_state, zeros_state, zeros_state), token_blocks)
    raw_all = raw_all.reshape(TOKENS, HEADS, HD)
    mean_sq = lax.optimization_barrier(jnp.mean(raw_all * raw_all, axis=-1, keepdims=True))
    normed = raw_all * lax.rsqrt(mean_sq + epsilon) * out_gain.reshape(HEADS, HD)
    return normed.reshape(TOKENS, HEADS * HD).astype(jnp.bfloat16)
```

```python
import functools

import jax
import jax.numpy as jnp
from jax import lax
from jax.experimental import pallas as pl
from jax.experimental.pallas import tpu as pltpu
from jax.sharding import Mesh, PartitionSpec as P

HD = 128
HALF = HD // 2
PACK = 96
ROWS = PACK + HD
epsilon = 1e-06
f32 = jnp.float32
bf16 = jnp.bfloat16
VM = pl.BlockSpec(memory_space=pltpu.VMEM)


def split(x):
    high = x.astype(bf16)
    return high, (x - high.astype(f32)).astype(bf16)


def mm2(a, b, ca, cb):
    dims = (((ca,), (cb,)), ((), ()))
    dot = lambda x, y: lax.dot_general(x, y, dims, preferred_element_type=f32)
    return dot(a[0], b[0]) + (dot(a[0], b[1]) + dot(a[1], b[0]))


def mm(a, b, ca=1, cb=0):
    return mm2(split(a), split(b), ca, cb)


def tril(x):
    n = x.shape[0]
    rows = lax.broadcasted_iota(jnp.int32, (n, n), 0)
    cols = lax.broadcasted_iota(jnp.int32, (n, n), 1)
    return jnp.where(rows >= cols, x, 0.0)


def pack_sym(s):
    low = jnp.concatenate([s[HALF:PACK, HALF:], s[PACK:, HALF:]], axis=1)
    return jnp.concatenate([s[:HALF], low], axis=0)


def unpack_sym(p):
    top = p[:HALF]
    corner = jnp.concatenate([p[HALF:, :HALF], p[HALF:, HALF:]], axis=0)
    low = jnp.concatenate([top[:, HALF:].T, corner], axis=1)
    return jnp.concatenate([top, low], axis=0)


def place():
    y = lax.axis_index("y")
    return lax.rem(y, 2), lax.axis_index("core")


def project_kernel(tok, own, other, q_ref, k_ref, v_ref, l_ref, blk_ref, pay_ref, wf):
    b, c = place()
    zs = own.shape[0]
    for z in range(zs):
        for f in range(2):
            near = 32 * (b if f == 0 else 1 - b)
            for part, ref in ((c, own), (1 - c, other)):
                at = pl.ds(pl.multiple_of(z * 128 + 64 * part + near, 32), 32)
                for ch in range(3):
                    wf[at, ch * HD : (ch + 1) * HD] = ref[z, f, ch]
    s_all = c_all = m_all = None
    for t in range(2):
        x = jnp.concatenate(
            [tok[(2 * (f % 2) + t) * 4 + f // 2] for f in range(8)], axis=1
        )
        proj = jnp.dot(x, wf[...], preferred_element_type=f32)
        q, k, v = proj[:, :HD], proj[:, HD : 2 * HD], proj[:, 2 * HD :]
        rows = slice(t * 256, t * 256 + 256)
        q_ref[rows], k_ref[rows], v_ref[rows] = q, k, v
        q2, k2, v2 = split(q), split(k), split(v)
        low = tril(mm2(q2, k2, 1, 1))
        l_ref[t] = low
        w = mm2(split(low), v2, 0, 0)
        s = mm2(k2, k2, 0, 0)
        cc = mm2(q2, v2, 0, 0)
        m = mm2(k2, split(w), 0, 0)
        if t == 0:
            s_all, c_all, m_all = s, cc, m
            blk_ref[0], blk_ref[1], blk_ref[2] = s, cc, m
        else:
            m_all = m_all + m + mm(s_all, cc)
            s_all, c_all = s_all + s, c_all + cc
    packed = pack_sym(s_all)
    for h in range(2):
        cols = slice(h * HALF, h * HALF + HALF)
        half = jnp.concatenate([c_all[:, cols], m_all[:, cols]], axis=1)
        for zb in range(2):
            pay_ref[2 * zb + h, :PACK] = packed
            pay_ref[2 * zb + h, PACK:] = half


def local_kernel(q_ref, v_ref, l_ref, blk_ref, raw_ref):
    for t in range(2):
        rows = slice(t * 256, t * 256 + 256)
        low = split(l_ref[t])
        pair = mm2(low, low, 1, 1)
        if t == 1:
            q2 = split(q_ref[rows])
            qs = mm2(q2, split(blk_ref[0]), 1, 0)
            pair = pair + mm2(split(qs), q2, 1, 1)
        raw = mm(tril(pair), v_ref[rows])
        if t == 1:
            raw = raw + mm2(q2, split(blk_ref[2]), 1, 0)
        raw_ref[rows] = raw


def pair_kernel(got, pay_ref, in_ref, s_in_ref):
    _, c = place()
    zb = lax.rem(lax.axis_index("z"), 2)
    pos = 2 * zb + c
    s = jnp.zeros((PACK, HD), f32)
    cm = jnp.zeros((HD, HD), f32)
    s_in = s
    before = [cm, cm]
    left = lax.broadcasted_iota(jnp.int32, (HD, HD), 1) < HALF
    for i in range(4):
        s_in = jnp.where(pos == i, s, s_in)
        before[i % 2] = jnp.where(zb == i // 2, cm, before[i % 2])
        new = got[i, PACK:]
        if i:
            cross = mm(unpack_sym(s), new[:, :HALF])
            cross = jnp.concatenate([jnp.zeros_like(cross), cross], axis=1)
            cm = cm + new + cross
        else:
            cm = new
        s = s + got[i, :PACK]
    pay_ref[:PACK] = s
    pay_ref[PACK:] = cm
    in_ref[0], in_ref[1] = before
    s_in_ref[...] = s_in


def prior_kernel(got, in_ref, s_in_ref, s_ref, keep_ref, send_ref):
    _, c = place()
    pair = lax.div(lax.axis_index("z"), 2)
    n = got.shape[0]
    s = jnp.zeros((PACK, HD), f32)
    m = jnp.zeros((HD, HALF), f32)
    lefts, rights = [], []
    for p in range(n - 1):
        live = p < pair
        if p:
            lefts.append(unpack_sym(s))
            rights.append(jnp.where(live, got[p, PACK:, :HALF], 0.0))
        m = m + jnp.where(live, got[p, PACK:, HALF:], 0.0)
        s = s + jnp.where(live, got[p, :PACK], 0.0)
    m = m + mm(jnp.concatenate(lefts, axis=1), jnp.concatenate(rights, axis=0))
    full = unpack_sym(s)
    both = jnp.concatenate([in_ref[0][:, :HALF], in_ref[1][:, :HALF]], axis=1)
    cross = mm(full, both)
    m0 = m + in_ref[0][:, HALF:] + cross[:, :HALF]
    m1 = m + in_ref[1][:, HALF:] + cross[:, HALF:]
    s_ref[...] = full + unpack_sym(s_in_ref[...])
    keep_ref[...] = jnp.where(c == 0, m0, m1)
    send_ref[...] = jnp.where(c == 0, m1, m0)


def cross_kernel(q_ref, v_ref, raw_ref, blk_ref, s_ref, out_ref):
    s2 = split(s_ref[...])
    for t in range(2):
        rows = slice(t * 256, t * 256 + 256)
        q2 = split(q_ref[rows])
        qs = split(mm2(q2, s2, 1, 0))
        scores = tril(mm2(qs, q2, 1, 1))
        raw = raw_ref[rows] + mm(scores, v_ref[rows])
        if t == 1:
            raw = raw + mm2(qs, split(blk_ref[1]), 1, 0)
        out_ref[rows] = raw


def final_kernel(q_ref, raw_ref, keep_ref, other_ref, gain_ref, gain_far_ref, out_ref):
    b, c = place()
    keep, other = keep_ref[...], other_ref[...]
    m2 = split(
        jnp.concatenate(
            [jnp.where(c == 0, keep, other), jnp.where(c == 0, other, keep)], axis=1
        )
    )
    y = lax.axis_index("y")
    gain = jnp.where(lax.div(y, 2) == c, gain_ref[...], gain_far_ref[...])
    gain = jnp.where(b == 0, gain[0:1], gain[1:2])
    for t in range(2):
        rows = slice(t * 256, t * 256 + 256)
        raw = raw_ref[rows] + mm2(split(q_ref[rows]), m2, 1, 0)
        mean_sq = jnp.mean(raw * raw, axis=-1, keepdims=True)
        out = raw * lax.rsqrt(mean_sq + epsilon) * gain
        out_ref[b if t == 0 else 1 - b] = out.astype(bf16)


def call(kernel, outs, flops, moved, scratch=()):
    return pl.pallas_call(
        kernel,
        out_shape=outs,
        scratch_shapes=list(scratch),
        compiler_params=pltpu.CompilerParams(vmem_limit_bytes=32 * 2**20),
        cost_estimate=pl.CostEstimate(flops=flops, bytes_accessed=moved, transcendentals=0),
    )


def swap_perm(flip):
    return [
        ((2 * a + b) * 2 + c, (2 * c + (b ^ flip)) * 2 + a)
        for a in range(2)
        for b in range(2)
        for c in range(2)
    ]


def body(zs, tokens, weight, gain):
    shape = jax.ShapeDtypeStruct
    b = lax.rem(lax.axis_index("y"), 2)
    yc = ("y", "core")
    first, second = weight[:, :, :HD], weight[:, :, HD:]
    same = jnp.where(b == 0, first, second).transpose(1, 0, 2)
    flip = jnp.where(b == 0, second, first).transpose(1, 0, 2)
    same = lax.ppermute(same, yc, swap_perm(0))
    flip = lax.ppermute(flip, yc, swap_perm(1))
    moved = lax.ppermute(tokens, yc, swap_perm(0))
    moved, same, flip = lax.optimization_barrier((moved, same, flip))
    everything = jnp.broadcast_to(moved[None], (16,) + moved.shape)
    tok = lax.all_to_all(everything, ("y", "x"), 0, 0)
    own = lax.all_gather(jnp.stack([same, flip]), "z")
    core_swap = [(0, 1), (1, 0)]
    other = lax.ppermute(own, "core", core_swap)
    rows = shape((512, HD), f32)
    mats = lambda n: shape((n, HD, HD), f32)
    q, k, v, low, blk, pay = call(
        project_kernel,
        (rows, rows, rows, shape((2, 256, 256), f32), mats(3), shape((4, ROWS, HD), f32)),
        1200 * 10**6,
        8 * 10**6,
        [pltpu.VMEM((zs * 128, 3 * HD), bf16)],
    )(tok, own, other)
    groups = [[(2 * p + i) * 2 + j for i in range(2) for j in range(2)] for p in range(zs // 2)]
    got = lax.all_to_all(pay, ("z", "core"), 0, 0, axis_index_groups=groups)
    gain, pay = lax.optimization_barrier((gain, pay))
    gain = gain.reshape(2, HD)
    gain_far = lax.ppermute(gain, "core", core_swap)
    raw = call(local_kernel, rows, 600 * 10**6, 4 * 10**6)(q, v, low, blk)
    total, inner, s_in = call(
        pair_kernel, (shape((ROWS, HD), f32), mats(2), shape((PACK, HD), f32)), 10**8, 10**6
    )(got)
    groups = [[2 * p + i for p in range(zs // 2)] for i in range(2)]
    totals = lax.all_gather(total, "z", axis_index_groups=groups)
    s, keep, send = call(
        prior_kernel, (shape((HD, HD), f32), shape((HD, HALF), f32), shape((HD, HALF), f32)), 10**8, 10**6
    )(totals, inner, s_in)
    other_m = lax.ppermute(send, "core", core_swap)
    raw = call(cross_kernel, rows, 500 * 10**6, 2 * 10**6)(q, v, raw, blk, s)
    out = call(final_kernel, shape((2, 256, HD), bf16), 10**8, 10**6)(
        q, raw, keep, other_m, gain, gain_far
    )
    near = lax.ppermute(out[0], yc, swap_perm(0))
    far = lax.ppermute(out[1], yc, swap_perm(1))
    left = jnp.where(b == 0, near, far)
    right = jnp.where(b == 0, far, near)
    return jnp.concatenate([left, right], axis=1)


def solution(mesh):
    zs = mesh.shape["ctx"] // 4
    fine = Mesh(mesh.devices.reshape(zs, 4, 4, 2), ("z", "y", "x", "core"))
    ctx, head = ("z", "y"), ("x", "core")
    return jax.shard_map(
        functools.partial(body, zs),
        mesh=fine,
        in_specs=(P(ctx, head), P(ctx, None, head), P(head)),
        out_specs=P(ctx, head),
        check_vma=False,
    )
```

```python
import functools

import jax
import jax.numpy as jnp
from jax import lax
from jax.experimental import pallas as pl
from jax.experimental.pallas import tpu as pltpu
from jax.sharding import Mesh, PartitionSpec as P

HD = 128
HALF = HD // 2
PACK = 96
ROWS = PACK + HD
epsilon = 1e-06
f32 = jnp.float32
bf16 = jnp.bfloat16
VM = pl.BlockSpec(memory_space=pltpu.VMEM)


def split(x):
    high = x.astype(bf16)
    return high, (x - high.astype(f32)).astype(bf16)


def mm2(a, b, ca, cb):
    dims = (((ca,), (cb,)), ((), ()))
    dot = lambda x, y: lax.dot_general(x, y, dims, preferred_element_type=f32)
    return dot(a[0], b[0]) + (dot(a[0], b[1]) + dot(a[1], b[0]))


def mm(a, b, ca=1, cb=0):
    return mm2(split(a), split(b), ca, cb)


def tril(x):
    n = x.shape[0]
    rows = lax.broadcasted_iota(jnp.int32, (n, n), 0)
    cols = lax.broadcasted_iota(jnp.int32, (n, n), 1)
    return jnp.where(rows >= cols, x, 0.0)


def pack_sym(s):
    low = jnp.concatenate([s[HALF:PACK, HALF:], s[PACK:, HALF:]], axis=1)
    return jnp.concatenate([s[:HALF], low], axis=0)


def unpack_sym(p):
    top = p[:HALF]
    corner = jnp.concatenate([p[HALF:, :HALF], p[HALF:, HALF:]], axis=0)
    low = jnp.concatenate([top[:, HALF:].T, corner], axis=1)
    return jnp.concatenate([top, low], axis=0)


def place():
    y = lax.axis_index("y")
    return lax.rem(y, 2), lax.axis_index("core")


def ring():
    return lax.rem(lax.axis_index("z") + lax.axis_index("core"), 2)


def ring_groups(zs):
    return [[z * 2 + (z + g) % 2 for z in range(zs)] for g in range(2)]


def project_kernel(mine, tok, own, out_ref, wf):
    b, c = place()
    half = c if mine else 1 - c
    for z in range(own.shape[0]):
        zh, z1, z0 = z // 4, z // 2 % 2, z % 2
        for f in range(2):
            near = 32 * (b if f == 0 else 1 - b)
            at = pl.ds(pl.multiple_of(zh * 256 + z0 * 128 + 64 * z1 + near, 32), 32)
            for ch in range(3):
                wf[at, ch * HD : (ch + 1) * HD] = own[z, f, ch]
    for t in range(2):
        x = jnp.concatenate([tok[8 * half + 4 * t + f] for f in range(4)], axis=1)
        out_ref[256 * t : 256 * t + 256] = jnp.dot(x, wf[...], preferred_element_type=f32)


def moment_kernel(keep, got, q_ref, k_ref, v_ref, blk_ref, pay_ref):
    for t in range(2):
        rows = slice(t * 256, t * 256 + 256)
        proj = keep[rows] + got[rows]
        q, k, v = proj[:, :HD], proj[:, HD : 2 * HD], proj[:, 2 * HD :]
        q_ref[rows], k_ref[rows], v_ref[rows] = q, k, v
        q2, k2, v2 = split(q), split(k), split(v)
        low = tril(mm2(q2, k2, 1, 1))
        w = mm2(split(low), v2, 0, 0)
        s = mm2(k2, k2, 0, 0)
        cc = mm2(q2, v2, 0, 0)
        m = mm2(k2, split(w), 0, 0)
        if t == 0:
            s_all, c_all, m_all = s, cc, m
            blk_ref[0], blk_ref[1], blk_ref[2] = s, cc, m
        else:
            m_all = m_all + m + mm(s_all, cc)
            s_all, c_all = s_all + s, c_all + cc
    packed = pack_sym(s_all)
    for h in range(2):
        cols = slice(h * HALF, h * HALF + HALF)
        half = jnp.concatenate([c_all[:, cols], m_all[:, cols]], axis=1)
        for zb in range(2):
            slot = 2 * zb + (zb + h) % 2
            pay_ref[slot, :PACK] = packed
            pay_ref[slot, PACK:] = half


def local_kernel(q_ref, k_ref, v_ref, blk_ref, raw_ref):
    for t in range(2):
        rows = slice(t * 256, t * 256 + 256)
        q2 = split(q_ref[rows])
        low = split(tril(mm2(q2, split(k_ref[rows]), 1, 1)))
        pair = mm2(low, low, 1, 1)
        if t == 1:
            qs = mm2(q2, split(blk_ref[0]), 1, 0)
            pair = pair + mm2(split(qs), q2, 1, 1)
        raw = mm(tril(pair), v_ref[rows])
        if t == 1:
            raw = raw + mm2(q2, split(blk_ref[2]), 1, 0)
        raw_ref[rows] = raw


def pair_kernel(got, pay_ref, in_ref, s_in_ref, all_ref):
    _, c = place()
    zb = lax.rem(lax.axis_index("z"), 2)
    pos = 2 * zb + c
    s = jnp.zeros((PACK, HD), f32)
    cm = jnp.zeros((HD, HD), f32)
    s_in = s
    before = [cm, cm]
    left = lax.broadcasted_iota(jnp.int32, (HD, HD), 1) < HALF
    for i in range(4):
        s_in = jnp.where(pos == i, s, s_in)
        before[i % 2] = jnp.where(zb == i // 2, cm, before[i % 2])
        new = got[i, PACK:]
        if i:
            cross = mm(unpack_sym(s), new[:, :HALF])
            cross = jnp.concatenate([jnp.zeros_like(cross), cross], axis=1)
            cm = cm + new + cross
        else:
            cm = new
        s = s + got[i, :PACK]
    all_ref[:PACK] = s
    all_ref[PACK:] = cm
    pay_ref[...] = all_ref[pl.ds(pl.multiple_of(zb * (ROWS // 2), 8), ROWS // 2)]
    in_ref[0], in_ref[1] = before
    s_in_ref[...] = s_in


def prior_kernel(got, in_ref, s_in_ref, s_ref, keep_ref, send_ref):
    _, c = place()
    pair = lax.div(lax.axis_index("z"), 2)
    n = got.shape[0]
    s = jnp.zeros((PACK, HD), f32)
    m = jnp.zeros((HD, HALF), f32)
    lefts, rights = [], []
    for p in range(n - 1):
        live = p < pair
        if p:
            lefts.append(unpack_sym(s))
            rights.append(jnp.where(live, got[p, PACK:, :HALF], 0.0))
        m = m + jnp.where(live, got[p, PACK:, HALF:], 0.0)
        s = s + jnp.where(live, got[p, :PACK], 0.0)
    m = m + mm(jnp.concatenate(lefts, axis=1), jnp.concatenate(rights, axis=0))
    full = unpack_sym(s)
    both = jnp.concatenate([in_ref[0][:, :HALF], in_ref[1][:, :HALF]], axis=1)
    cross = mm(full, both)
    m0 = m + in_ref[0][:, HALF:] + cross[:, :HALF]
    m1 = m + in_ref[1][:, HALF:] + cross[:, HALF:]
    s_ref[...] = full + unpack_sym(s_in_ref[...])
    keep_ref[...] = jnp.where(c == 0, m0, m1)
    send_ref[...] = jnp.where(c == 0, m1, m0)


def cross_kernel(q_ref, v_ref, raw_ref, blk_ref, s_ref, out_ref):
    s2 = split(s_ref[...])
    for t in range(2):
        rows = slice(t * 256, t * 256 + 256)
        q2 = split(q_ref[rows])
        qs = split(mm2(q2, s2, 1, 0))
        scores = tril(mm2(qs, q2, 1, 1))
        raw = raw_ref[rows] + mm(scores, v_ref[rows])
        if t == 1:
            raw = raw + mm2(qs, split(blk_ref[1]), 1, 0)
        out_ref[rows] = raw


def final_kernel(q_ref, raw_ref, keep_ref, other_ref, gain_ref, gain_far_ref, near_ref, far_ref):
    b, c = place()
    h = ring()
    keep, other = keep_ref[...], other_ref[...]
    m2 = split(
        jnp.concatenate(
            [jnp.where(h == 0, keep, other), jnp.where(h == 0, other, keep)], axis=1
        )
    )
    y = lax.axis_index("y")
    gain = jnp.where(lax.div(y, 2) == c, gain_ref[...], gain_far_ref[...])
    gain = jnp.where(b == 0, gain[0:1], gain[1:2])
    for t in range(2):
        rows = slice(t * 256, t * 256 + 256)
        raw = raw_ref[rows] + mm2(split(q_ref[rows]), m2, 1, 0)
        mean_sq = jnp.mean(raw * raw, axis=-1, keepdims=True)
        out = (raw * lax.rsqrt(mean_sq + epsilon) * gain).astype(bf16)

        @pl.when(b == t)
        def _():
            near_ref[...] = out

        @pl.when(b != t)
        def _():
            far_ref[...] = out


def call(kernel, outs, flops, moved, scratch=()):
    return pl.pallas_call(
        kernel,
        out_shape=outs,
        scratch_shapes=list(scratch),
        compiler_params=pltpu.CompilerParams(vmem_limit_bytes=32 * 2**20),
        cost_estimate=pl.CostEstimate(flops=flops, bytes_accessed=moved, transcendentals=0),
    )


def pair_swap(flip):
    return [
        ((2 * a + b) * 2 + c, (2 * c + (b ^ flip)) * 2 + a)
        for a in range(2)
        for b in range(2)
        for c in range(2)
    ]


def weight_perm(zs, flip):
    pairs = []
    for z in range(zs):
        zh, z1, z0 = z // 4, z // 2 % 2, z % 2
        for y in range(4):
            a, b = y // 2, y % 2
            for c in range(2):
                to = (4 * zh + 2 * a + z0) * 8 + (2 * c + (b ^ flip)) * 2 + (z1 ^ z0)
                pairs.append((z * 8 + y * 2 + c, to))
    return pairs


def body(zs, tokens, weight, gain):
    shape = jax.ShapeDtypeStruct
    b = lax.rem(lax.axis_index("y"), 2)
    yc, zyc = ("y", "core"), ("z", "y", "core")
    core_swap = [(0, 1), (1, 0)]
    rows, mats = shape((512, HD), f32), lambda n: shape((n, HD, HD), f32)
    wide = shape((512, 3 * HD), f32)
    first, second = weight[:, :, :HD], weight[:, :, HD:]
    same = jnp.where(b == 0, first, second).transpose(1, 0, 2)
    flip = jnp.where(b == 0, second, first).transpose(1, 0, 2)
    same = lax.ppermute(same, zyc, weight_perm(zs, 0))
    flip = lax.ppermute(flip, zyc, weight_perm(zs, 1))
    turn = [(z * 2 + c, z * 2 + (c ^ z % 2)) for z in range(zs) for c in range(2)]
    tokens = lax.ppermute(tokens, ("z", "core"), turn)
    everything = jnp.broadcast_to(tokens[None], (16,) + tokens.shape)
    everything, same, flip = lax.optimization_barrier((everything, same, flip))
    tok = lax.all_to_all(everything, ("y", "x"), 0, 0)
    own = lax.all_gather(
        jnp.stack([same, flip]), ("z", "core"), axis_index_groups=ring_groups(zs)
    )
    scratch = [pltpu.VMEM((zs * 64, 3 * HD), bf16)]
    send = call(functools.partial(project_kernel, False), wide, 400 * 10**6, 3 * 10**6, scratch)(tok, own)
    got = lax.ppermute(send, "core", core_swap)
    keep = call(functools.partial(project_kernel, True), wide, 400 * 10**6, 3 * 10**6, scratch)(tok, own)
    q, k, v, blk, pay = call(
        moment_kernel,
        (rows, rows, rows, mats(3), shape((4, ROWS, HD), f32)),
        600 * 10**6,
        3 * 10**6,
    )(keep, got)
    groups = [[(2 * p + i) * 2 + j for i in range(2) for j in range(2)] for p in range(zs // 2)]
    got = lax.all_to_all(pay, ("z", "core"), 0, 0, axis_index_groups=groups)
    gain, pay = lax.optimization_barrier((gain, pay))
    gain = gain.reshape(2, HD)
    gain_far = lax.ppermute(gain, "core", core_swap)
    raw = call(local_kernel, rows, 800 * 10**6, 2 * 10**6)(q, k, v, blk)
    total, inner, s_in = call(
        pair_kernel,
        (shape((ROWS // 2, HD), f32), mats(2), shape((PACK, HD), f32)),
        10**8,
        10**6,
        [pltpu.VMEM((ROWS, HD), f32)],
    )(got)
    totals = lax.all_gather(total, ("z", "core"), axis_index_groups=ring_groups(zs))
    totals = totals.reshape(zs // 2, ROWS, HD)
    s, keep, send = call(
        prior_kernel, (shape((HD, HD), f32), shape((HD, HALF), f32), shape((HD, HALF), f32)), 10**8, 10**6
    )(totals, inner, s_in)
    other_m = lax.ppermute(send, "core", core_swap)
    raw = call(cross_kernel, rows, 500 * 10**6, 2 * 10**6)(q, v, raw, blk, s)
    half = shape((256, HD), bf16)
    near, far = call(final_kernel, (half, half), 10**8, 10**6)(q, raw, keep, other_m, gain, gain_far)
    near = lax.ppermute(near, yc, pair_swap(0))
    far = lax.ppermute(far, yc, pair_swap(1))
    left = jnp.where(b == 0, near, far)
    right = jnp.where(b == 0, far, near)
    return jnp.concatenate([left, right], axis=1)


def solution(mesh):
    zs = mesh.shape["ctx"] // 4
    fine = Mesh(mesh.devices.reshape(zs, 4, 4, 2), ("z", "y", "x", "core"))
    ctx, head = ("z", "y"), ("x", "core")
    return jax.shard_map(
        functools.partial(body, zs),
        mesh=fine,
        in_specs=(P(ctx, head), P(ctx, None, head), P(head)),
        out_specs=P(ctx, head),
        check_vma=False,
    )
```

```python
import functools

import jax
import jax.numpy as jnp
from jax import lax
from jax.experimental import pallas as pl
from jax.experimental.pallas import tpu as pltpu
from jax.sharding import Mesh, PartitionSpec as P


HD = 128
HALF = HD // 2
PACK = 72
ROWS = PACK + HD
PART = 104
epsilon = 1e-06
f32 = jnp.float32
bf16 = jnp.bfloat16
VM = pl.BlockSpec(memory_space=pltpu.VMEM)


def split(x):
    high = x.astype(bf16)
    return high, (x - high.astype(f32)).astype(bf16)


def mm2(a, b, ca, cb):
    dims = (((ca,), (cb,)), ((), ()))
    dot = lambda x, y: lax.dot_general(x, y, dims, preferred_element_type=f32)
    return dot(a[0], b[0]) + (dot(a[0], b[1]) + dot(a[1], b[0]))


def mm(a, b, ca=1, cb=0):
    return mm2(split(a), split(b), ca, cb)


def dot(x, y, ca=1, cb=0):
    return lax.dot_general(x, y, (((ca,), (cb,)), ((), ())), preferred_element_type=f32)


def left3(x):
    return jnp.concatenate([x[0], x[0], x[1]], axis=1)


def right3(y, axis):
    return jnp.concatenate([y[0], y[1], y[0]], axis=axis)


def narrow(x, y, cy=0):
    return dot(left3(x), right3(y, cy), 1, cy)


def wide(x, y):
    both = dot(x[0], jnp.concatenate([y[0], y[1]], axis=1))
    return both[:, :HD] + both[:, HD:] + dot(x[1], y[0])


def tril(x):
    n = x.shape[0]
    rows = lax.broadcasted_iota(jnp.int32, (n, n), 0)
    cols = lax.broadcasted_iota(jnp.int32, (n, n), 1)
    return jnp.where(rows >= cols, x, 0.0)


def corner_ids():
    rows = lax.broadcasted_iota(jnp.int32, (HALF, HALF), 0)
    return rows, lax.broadcasted_iota(jnp.int32, (HALF, HALF), 1)


def triu(x):
    n = x.shape[0]
    rows = lax.broadcasted_iota(jnp.int32, (n, n), 0)
    cols = lax.broadcasted_iota(jnp.int32, (n, n), 1)
    return jnp.where(rows <= cols, x, 0.0)


def pack_sym(s):
    rows, cols = corner_ids()
    a, b, d = s[:HALF, :HALF], s[:HALF, HALF:], s[HALF:, HALF:]
    diag = jnp.sum(jnp.where(rows == cols, d, 0.0), axis=0, keepdims=True)
    diag = jnp.broadcast_to(jnp.concatenate([diag, diag], axis=1), (PACK - HALF, HD))
    return jnp.concatenate([jnp.concatenate([b, jnp.where(rows <= cols, a, d)], axis=1), diag], axis=0)


def unpack_sym(p):
    rows, cols = corner_ids()
    b, tri = p[:HALF, :HALF], p[:HALF, HALF:]
    flip = tri.T
    a = jnp.where(rows <= cols, tri, flip)
    d = jnp.where(rows > cols, tri, flip)
    d = jnp.where(rows == cols, p[HALF : HALF + 1, :HALF], d)
    return jnp.concatenate(
        [jnp.concatenate([a, b], axis=1), jnp.concatenate([b.T, d], axis=1)], axis=0
    )


def place():
    y = lax.axis_index("y")
    return lax.rem(y, 2), lax.axis_index("core")


def ring():
    return lax.rem(lax.axis_index("z") + lax.axis_index("core"), 2)


def ring_groups(zs):
    return [[z * 2 + (z + g) % 2 for z in range(zs)] for g in range(2)]


def project_kernel(mine, tok, own, out_ref, wf):
    b, c = place()
    half = c if mine else 1 - c
    for z in range(own.shape[0]):
        zh, z1, z0 = z // 4, z // 2 % 2, z % 2
        for f in range(2):
            near = 32 * (b if f == 0 else 1 - b)
            at = pl.ds(pl.multiple_of(zh * 256 + z0 * 128 + 64 * z1 + near, 32), 32)
            for ch in range(3):
                wf[at, ch * HD : (ch + 1) * HD] = own[z, f, ch]
    for t in range(2):
        x = jnp.concatenate([tok[4 * f + 2 * half + t] for f in range(4)], axis=1)
        out_ref[256 * t : 256 * t + 256] = jnp.dot(x, wf[...], preferred_element_type=f32)


def moment_kernel(keep, got, q_ref, k_ref, v_ref, blk_ref, pay_ref):
    for t in range(2):
        rows = slice(t * 256, t * 256 + 256)
        proj = keep[rows] + got[rows]
        q, k, v = proj[:, :HD], proj[:, HD : 2 * HD], proj[:, 2 * HD :]
        q_ref[rows], k_ref[rows], v_ref[rows] = q, k, v
        q2, k2, v2 = split(q), split(k), split(v)
        w2 = split(wide(split(triu(narrow(k2, q2, 1))), v2))
        kh, kl = k2[0].T, k2[1].T
        a = dot(kh, jnp.concatenate([k2[0], k2[1], w2[0], w2[1]], axis=1))
        d = dot(kl, jnp.concatenate([k2[0], w2[0]], axis=1))
        s = a[:, :HD] + a[:, HD : 2 * HD] + d[:, :HD]
        m = a[:, 2 * HD : 3 * HD] + a[:, 3 * HD :] + d[:, HD:]
        cc = wide((q2[0].T, q2[1].T), v2)
        if t == 0:
            s_all, c_all, m_all = s, cc, m
            blk_ref[0], blk_ref[1], blk_ref[2] = s, cc, m
        else:
            m_all = m_all + m + narrow(split(s_all), split(cc))
            s_all, c_all = s_all + s, c_all + cc
    packed = pack_sym(s_all)
    for h in range(2):
        cols = slice(h * HALF, h * HALF + HALF)
        half = jnp.concatenate([c_all[:, cols], m_all[:, cols]], axis=1)
        for zb in range(2):
            slot = 2 * zb + (zb + h) % 2
            pay_ref[slot, :PACK] = packed
            pay_ref[slot, PACK:] = half


def local_kernel(q_ref, k_ref, v_ref, blk_ref, raw_ref):
    for t in range(2):
        rows = slice(t * 256, t * 256 + 256)
        q2 = split(q_ref[rows])
        low = split(tril(narrow(q2, split(k_ref[rows]), 1)))
        pair = mm2(low, low, 1, 1)
        if t == 1:
            qs = narrow(q2, split(blk_ref[0]))
            pair = pair + narrow(split(qs), q2, 1)
        raw = wide(split(tril(pair)), split(v_ref[rows]))
        if t == 1:
            raw = raw + narrow(q2, split(blk_ref[2]))
        raw_ref[rows] = raw


def pair_kernel(got, pay_ref, in_ref, s_in_ref, all_ref):
    _, c = place()
    zb = lax.rem(lax.axis_index("z"), 2)
    pos = 2 * zb + c
    s = jnp.zeros((PACK, HD), f32)
    cm = jnp.zeros((HD, HD), f32)
    s_in = s
    before = [cm, cm]
    left = lax.broadcasted_iota(jnp.int32, (HD, HD), 1) < HALF
    for i in range(4):
        s_in = jnp.where(pos == i, s, s_in)
        before[i % 2] = jnp.where(zb == i // 2, cm, before[i % 2])
        new = got[i, PACK:]
        if i:
            cross = mm(unpack_sym(s), new[:, :HALF])
            cross = jnp.concatenate([jnp.zeros_like(cross), cross], axis=1)
            cm = cm + new + cross
        else:
            cm = new
        s = s + got[i, :PACK]
    all_ref[:PACK] = s
    all_ref[PACK:ROWS] = cm
    all_ref[ROWS:] = jnp.zeros((2 * PART - ROWS, HD), f32)
    pay_ref[...] = all_ref[pl.ds(pl.multiple_of(zb * PART, 8), PART)]
    in_ref[0], in_ref[1] = before
    s_in_ref[...] = s_in


def prior_kernel(got, in_ref, s_in_ref, s_ref, keep_ref, send_ref):
    _, c = place()
    pair = lax.div(lax.axis_index("z"), 2)
    n = got.shape[0]
    s = jnp.zeros((PACK, HD), f32)
    m = jnp.zeros((HD, HALF), f32)
    lefts, rights = [], []
    for p in range(n - 1):
        live = p < pair
        if p:
            lefts.append(unpack_sym(s))
            rights.append(jnp.where(live, got[p, PACK:ROWS, :HALF], 0.0))
        m = m + jnp.where(live, got[p, PACK:ROWS, HALF:], 0.0)
        s = s + jnp.where(live, got[p, :PACK], 0.0)
    m = m + mm(jnp.concatenate(lefts, axis=1), jnp.concatenate(rights, axis=0))
    full = unpack_sym(s)
    both = jnp.concatenate([in_ref[0][:, :HALF], in_ref[1][:, :HALF]], axis=1)
    cross = mm(full, both)
    m0 = m + in_ref[0][:, HALF:] + cross[:, :HALF]
    m1 = m + in_ref[1][:, HALF:] + cross[:, HALF:]
    s_ref[...] = full + unpack_sym(s_in_ref[...])
    keep_ref[...] = jnp.where(c == 0, m0, m1)
    send_ref[...] = jnp.where(c == 0, m1, m0)


def cross_kernel(q_ref, v_ref, raw_ref, blk_ref, s_ref, out_ref):
    s2 = split(s_ref[...])
    for t in range(2):
        rows = slice(t * 256, t * 256 + 256)
        q2 = split(q_ref[rows])
        qs = split(narrow(q2, s2))
        scores = tril(narrow(qs, q2, 1))
        raw = raw_ref[rows] + wide(split(scores), split(v_ref[rows]))
        if t == 1:
            raw = raw + narrow(qs, split(blk_ref[1]))
        out_ref[rows] = raw


def final_kernel(q_ref, raw_ref, keep_ref, other_ref, gain_ref, gain_far_ref, near_ref, far_ref):
    b, c = place()
    h = ring()
    keep, other = keep_ref[...], other_ref[...]
    m2 = split(
        jnp.concatenate(
            [jnp.where(h == 0, keep, other), jnp.where(h == 0, other, keep)], axis=1
        )
    )
    y = lax.axis_index("y")
    gain = jnp.where(lax.div(y, 2) == c, gain_ref[...], gain_far_ref[...])
    gain = jnp.where(b == 0, gain[0:1], gain[1:2])
    for t in range(2):
        rows = slice(t * 256, t * 256 + 256)
        raw = raw_ref[rows] + narrow(split(q_ref[rows]), m2)
        mean_sq = jnp.mean(raw * raw, axis=-1, keepdims=True)
        out = (raw * lax.rsqrt(mean_sq + epsilon) * gain).astype(bf16)

        @pl.when(b == t)
        def _():
            near_ref[...] = out

        @pl.when(b != t)
        def _():
            far_ref[...] = out


def call(kernel, outs, flops, moved, scratch=()):
    return pl.pallas_call(
        kernel,
        out_shape=outs,
        scratch_shapes=list(scratch),
        compiler_params=pltpu.CompilerParams(vmem_limit_bytes=32 * 2**20),
        cost_estimate=pl.CostEstimate(flops=flops, bytes_accessed=moved, transcendentals=0),
    )


def pair_swap(flip):
    return [
        ((2 * a + b) * 2 + c, (2 * c + (b ^ flip)) * 2 + a)
        for a in range(2)
        for b in range(2)
        for c in range(2)
    ]


def weight_perm(zs, flip):
    pairs = []
    for z in range(zs):
        zh, z1, z0 = z // 4, z // 2 % 2, z % 2
        for y in range(4):
            a, b = y // 2, y % 2
            for c in range(2):
                to = (4 * zh + 2 * a + z0) * 8 + (2 * c + (b ^ flip)) * 2 + (z1 ^ z0)
                pairs.append((z * 8 + y * 2 + c, to))
    return pairs


def body(zs, tokens, weight, gain):
    shape = jax.ShapeDtypeStruct
    b = lax.rem(lax.axis_index("y"), 2)
    yc, zyc = ("y", "core"), ("z", "y", "core")
    core_swap = [(0, 1), (1, 0)]
    rows, mats = shape((512, HD), f32), lambda n: shape((n, HD, HD), f32)
    wide = shape((512, 3 * HD), f32)
    first, second = weight[:, :, :HD], weight[:, :, HD:]
    same = jnp.where(b == 0, first, second).transpose(1, 0, 2)
    flip = jnp.where(b == 0, second, first).transpose(1, 0, 2)
    same = lax.ppermute(same, zyc, weight_perm(zs, 0))
    flip = lax.ppermute(flip, zyc, weight_perm(zs, 1))
    turn = [(z * 2 + c, z * 2 + (c ^ z % 2)) for z in range(zs) for c in range(2)]
    tokens = lax.ppermute(tokens, ("z", "core"), turn)
    tok = lax.all_to_all(jnp.broadcast_to(tokens[None], (16,) + tokens.shape), ("x", "y"), 0, 0)
    own = lax.all_gather(
        jnp.stack([same, flip]), ("z", "core"), axis_index_groups=ring_groups(zs)
    )
    scratch = [pltpu.VMEM((zs * 64, 3 * HD), bf16)]
    send = call(functools.partial(project_kernel, False), wide, 400 * 10**6, 3 * 10**6, scratch)(tok, own)
    got = lax.ppermute(send, "core", core_swap)
    keep = call(functools.partial(project_kernel, True), wide, 400 * 10**6, 3 * 10**6, scratch)(tok, own)
    q, k, v, blk, pay = call(
        moment_kernel,
        (rows, rows, rows, mats(3), shape((4, ROWS, HD), f32)),
        600 * 10**6,
        3 * 10**6,
    )(keep, got)
    groups = [[(2 * p + i) * 2 + j for i in range(2) for j in range(2)] for p in range(zs // 2)]
    got = lax.all_to_all(pay, ("z", "core"), 0, 0, axis_index_groups=groups)
    gain, pay = lax.optimization_barrier((gain, pay))
    gain = gain.reshape(2, HD)
    gain_far = lax.ppermute(gain, "core", core_swap)
    raw = call(local_kernel, rows, 800 * 10**6, 2 * 10**6)(q, k, v, blk)
    total, inner, s_in = call(
        pair_kernel,
        (shape((PART, HD), f32), mats(2), shape((PACK, HD), f32)),
        10**8,
        10**6,
        [pltpu.VMEM((2 * PART, HD), f32)],
    )(got)
    totals = lax.all_gather(total, ("z", "core"), axis_index_groups=ring_groups(zs))
    totals = totals.reshape(zs // 2, 2 * PART, HD)
    s, keep, send = call(
        prior_kernel, (shape((HD, HD), f32), shape((HD, HALF), f32), shape((HD, HALF), f32)), 10**8, 10**6
    )(totals, inner, s_in)
    other_m = lax.ppermute(send, "core", core_swap)
    raw = call(cross_kernel, rows, 500 * 10**6, 2 * 10**6)(q, v, raw, blk, s)
    half = shape((256, HD), bf16)
    near, far = call(final_kernel, (half, half), 10**8, 10**6)(q, raw, keep, other_m, gain, gain_far)
    near = lax.ppermute(near, yc, pair_swap(0))
    far = lax.ppermute(far, yc, pair_swap(1))
    left = jnp.where(b == 0, near, far)
    right = jnp.where(b == 0, far, near)
    return jnp.concatenate([left, right], axis=1)


def solution(mesh):
    zs = mesh.shape["ctx"] // 4
    fine = Mesh(mesh.devices.reshape(zs, 4, 4, 2), ("z", "y", "x", "core"))
    ctx, head = ("z", "y"), ("x", "core")
    return jax.shard_map(
        functools.partial(body, zs),
        mesh=fine,
        in_specs=(P(ctx, head), P(ctx, None, head), P(head)),
        out_specs=P(ctx, head),
        check_vma=False,
    )
```

```python
import functools

import jax
import jax.numpy as jnp
from jax import lax
from jax.experimental import pallas as pl
from jax.experimental.pallas import tpu as pltpu
from jax.sharding import Mesh, PartitionSpec as P


HD = 128
HALF = HD // 2
PACK = 72
ROWS = PACK + HD
PART = 104
epsilon = 1e-06
f32 = jnp.float32
bf16 = jnp.bfloat16
VM = pl.BlockSpec(memory_space=pltpu.VMEM)


def split(x):
    high = x.astype(bf16)
    return high, (x - high.astype(f32)).astype(bf16)


def mm2(a, b, ca, cb):
    dims = (((ca,), (cb,)), ((), ()))
    dot = lambda x, y: lax.dot_general(x, y, dims, preferred_element_type=f32)
    return dot(a[0], b[0]) + (dot(a[0], b[1]) + dot(a[1], b[0]))


def mm(a, b, ca=1, cb=0):
    return mm2(split(a), split(b), ca, cb)


def dot(x, y, ca=1, cb=0):
    return lax.dot_general(x, y, (((ca,), (cb,)), ((), ())), preferred_element_type=f32)


def left3(x):
    return jnp.concatenate([x[0], x[0], x[1]], axis=1)


def right3(y, axis):
    return jnp.concatenate([y[0], y[1], y[0]], axis=axis)


def narrow(x, y, cy=0):
    return dot(left3(x), right3(y, cy), 1, cy)


def wide(x, y):
    both = dot(x[0], jnp.concatenate([y[0], y[1]], axis=1))
    return both[:, :HD] + both[:, HD:] + dot(x[1], y[0])


def tril(x):
    n = x.shape[0]
    rows = lax.broadcasted_iota(jnp.int32, (n, n), 0)
    cols = lax.broadcasted_iota(jnp.int32, (n, n), 1)
    return jnp.where(rows >= cols, x, 0.0)


def corner_ids():
    rows = lax.broadcasted_iota(jnp.int32, (HALF, HALF), 0)
    return rows, lax.broadcasted_iota(jnp.int32, (HALF, HALF), 1)


def triu(x):
    n = x.shape[0]
    rows = lax.broadcasted_iota(jnp.int32, (n, n), 0)
    cols = lax.broadcasted_iota(jnp.int32, (n, n), 1)
    return jnp.where(rows <= cols, x, 0.0)


def pack_sym(s):
    rows, cols = corner_ids()
    a, b, d = s[:HALF, :HALF], s[:HALF, HALF:], s[HALF:, HALF:]
    diag = jnp.sum(jnp.where(rows == cols, d, 0.0), axis=0, keepdims=True)
    diag = jnp.broadcast_to(jnp.concatenate([diag, diag], axis=1), (PACK - HALF, HD))
    return jnp.concatenate([jnp.concatenate([b, jnp.where(rows <= cols, a, d)], axis=1), diag], axis=0)


def unpack_sym(p):
    rows, cols = corner_ids()
    b, tri = p[:HALF, :HALF], p[:HALF, HALF:]
    flip = tri.T
    a = jnp.where(rows <= cols, tri, flip)
    d = jnp.where(rows > cols, tri, flip)
    d = jnp.where(rows == cols, p[HALF : HALF + 1, :HALF], d)
    return jnp.concatenate(
        [jnp.concatenate([a, b], axis=1), jnp.concatenate([b.T, d], axis=1)], axis=0
    )


def place():
    y = lax.axis_index("y")
    return lax.rem(y, 2), lax.axis_index("core")


def ring():
    return lax.rem(lax.axis_index("z") + lax.axis_index("core"), 2)


def ring_groups(zs):
    return [[z * 2 + (z + g) % 2 for z in range(zs)] for g in range(2)]


def halve_kernel(tok, keep_ref, send_ref):
    h = ring()
    left, right = tok[:, :HD], tok[:, HD:]
    even = jnp.concatenate([left[:, :HALF], right[:, :HALF]], axis=1)
    odd = jnp.concatenate([left[:, HALF:], right[:, HALF:]], axis=1)
    keep_ref[...] = jnp.where(h == 0, even, odd)
    send_ref[...] = jnp.where(h == 0, odd, even)


def project_kernel(mine, tok, own, out_ref, wf):
    b, c = place()
    half = c if mine else 1 - c
    for z in range(own.shape[0]):
        zh, z1, z0 = z // 4, z // 2 % 2, z % 2
        side = 128 * (c if z1 == 0 else 1 - c)
        for f in range(2):
            near = 32 * (b if f == 0 else 1 - b)
            at = pl.ds(pl.multiple_of(zh * 256 + 64 * z0 + side + near, 32), 32)
            for ch in range(3):
                wf[at, ch * HD : (ch + 1) * HD] = own[z, f, ch]
    for t in range(2):
        pieces = [(4 * f + 2 * half + t, side) for f in range(4) for side in range(2)]
        x = jnp.concatenate([tok[slot, side] for slot, side in pieces], axis=1)
        out_ref[256 * t : 256 * t + 256] = jnp.dot(x, wf[...], preferred_element_type=f32)


def moment_kernel(keep, got, q_ref, k_ref, v_ref, blk_ref, pay_ref):
    for t in range(2):
        rows = slice(t * 256, t * 256 + 256)
        proj = keep[rows] + got[rows]
        q, k, v = proj[:, :HD], proj[:, HD : 2 * HD], proj[:, 2 * HD :]
        q_ref[rows], k_ref[rows], v_ref[rows] = q, k, v
        q2, k2, v2 = split(q), split(k), split(v)
        w2 = split(wide(split(triu(narrow(k2, q2, 1))), v2))
        kh, kl = k2[0].T, k2[1].T
        a = dot(kh, jnp.concatenate([k2[0], k2[1], w2[0], w2[1]], axis=1))
        d = dot(kl, jnp.concatenate([k2[0], w2[0]], axis=1))
        s = a[:, :HD] + a[:, HD : 2 * HD] + d[:, :HD]
        m = a[:, 2 * HD : 3 * HD] + a[:, 3 * HD :] + d[:, HD:]
        cc = wide((q2[0].T, q2[1].T), v2)
        if t == 0:
            s_all, c_all, m_all = s, cc, m
            blk_ref[0], blk_ref[1], blk_ref[2] = s, cc, m
        else:
            m_all = m_all + m + narrow(split(s_all), split(cc))
            s_all, c_all = s_all + s, c_all + cc
    packed = pack_sym(s_all)
    for h in range(2):
        cols = slice(h * HALF, h * HALF + HALF)
        half = jnp.concatenate([c_all[:, cols], m_all[:, cols]], axis=1)
        for zb in range(2):
            slot = 2 * zb + (zb + h) % 2
            pay_ref[slot, :PACK] = packed
            pay_ref[slot, PACK:] = half


def local_kernel(q_ref, k_ref, v_ref, blk_ref, raw_ref):
    for t in range(2):
        rows = slice(t * 256, t * 256 + 256)
        q2 = split(q_ref[rows])
        low = split(tril(narrow(q2, split(k_ref[rows]), 1)))
        pair = mm2(low, low, 1, 1)
        if t == 1:
            qs = narrow(q2, split(blk_ref[0]))
            pair = pair + narrow(split(qs), q2, 1)
        raw = wide(split(tril(pair)), split(v_ref[rows]))
        if t == 1:
            raw = raw + narrow(q2, split(blk_ref[2]))
        raw_ref[rows] = raw


def pair_kernel(got, pay_ref, in_ref, s_in_ref, all_ref):
    _, c = place()
    zb = lax.rem(lax.axis_index("z"), 2)
    pos = 2 * zb + c
    s = jnp.zeros((PACK, HD), f32)
    cm = jnp.zeros((HD, HD), f32)
    s_in = s
    before = [cm, cm]
    left = lax.broadcasted_iota(jnp.int32, (HD, HD), 1) < HALF
    for i in range(4):
        s_in = jnp.where(pos == i, s, s_in)
        before[i % 2] = jnp.where(zb == i // 2, cm, before[i % 2])
        new = got[i, PACK:]
        if i:
            cross = mm(unpack_sym(s), new[:, :HALF])
            cross = jnp.concatenate([jnp.zeros_like(cross), cross], axis=1)
            cm = cm + new + cross
        else:
            cm = new
        s = s + got[i, :PACK]
    all_ref[:PACK] = s
    all_ref[PACK:ROWS] = cm
    all_ref[ROWS:] = jnp.zeros((2 * PART - ROWS, HD), f32)
    pay_ref[...] = all_ref[pl.ds(pl.multiple_of(zb * PART, 8), PART)]
    in_ref[0], in_ref[1] = before
    s_in_ref[...] = s_in


def prior_kernel(got, in_ref, s_in_ref, s_ref, keep_ref, send_ref):
    _, c = place()
    pair = lax.div(lax.axis_index("z"), 2)
    n = got.shape[0]
    s = jnp.zeros((PACK, HD), f32)
    m = jnp.zeros((HD, HALF), f32)
    lefts, rights = [], []
    for p in range(n - 1):
        live = p < pair
        if p:
            lefts.append(unpack_sym(s))
            rights.append(jnp.where(live, got[p, PACK:ROWS, :HALF], 0.0))
        m = m + jnp.where(live, got[p, PACK:ROWS, HALF:], 0.0)
        s = s + jnp.where(live, got[p, :PACK], 0.0)
    m = m + mm(jnp.concatenate(lefts, axis=1), jnp.concatenate(rights, axis=0))
    full = unpack_sym(s)
    both = jnp.concatenate([in_ref[0][:, :HALF], in_ref[1][:, :HALF]], axis=1)
    cross = mm(full, both)
    m0 = m + in_ref[0][:, HALF:] + cross[:, :HALF]
    m1 = m + in_ref[1][:, HALF:] + cross[:, HALF:]
    s_ref[...] = full + unpack_sym(s_in_ref[...])
    keep_ref[...] = jnp.where(c == 0, m0, m1)
    send_ref[...] = jnp.where(c == 0, m1, m0)


def cross_kernel(q_ref, v_ref, raw_ref, blk_ref, s_ref, out_ref):
    s2 = split(s_ref[...])
    for t in range(2):
        rows = slice(t * 256, t * 256 + 256)
        q2 = split(q_ref[rows])
        qs = split(narrow(q2, s2))
        scores = tril(narrow(qs, q2, 1))
        raw = raw_ref[rows] + wide(split(scores), split(v_ref[rows]))
        if t == 1:
            raw = raw + narrow(qs, split(blk_ref[1]))
        out_ref[rows] = raw


def final_kernel(q_ref, raw_ref, keep_ref, other_ref, gain_ref, gain_far_ref, near_ref, far_ref):
    b, c = place()
    h = ring()
    keep, other = keep_ref[...], other_ref[...]
    m2 = split(
        jnp.concatenate(
            [jnp.where(h == 0, keep, other), jnp.where(h == 0, other, keep)], axis=1
        )
    )
    y = lax.axis_index("y")
    gain = jnp.where(lax.div(y, 2) == c, gain_ref[...], gain_far_ref[...])
    gain = jnp.where(b == 0, gain[0:1], gain[1:2])
    for t in range(2):
        rows = slice(t * 256, t * 256 + 256)
        raw = raw_ref[rows] + narrow(split(q_ref[rows]), m2)
        mean_sq = jnp.mean(raw * raw, axis=-1, keepdims=True)
        out = (raw * lax.rsqrt(mean_sq + epsilon) * gain).astype(bf16)

        @pl.when(b == t)
        def _():
            near_ref[...] = out

        @pl.when(b != t)
        def _():
            far_ref[...] = out


def call(kernel, outs, flops, moved, scratch=()):
    return pl.pallas_call(
        kernel,
        out_shape=outs,
        scratch_shapes=list(scratch),
        compiler_params=pltpu.CompilerParams(vmem_limit_bytes=32 * 2**20),
        cost_estimate=pl.CostEstimate(flops=flops, bytes_accessed=moved, transcendentals=0),
    )


def pair_swap(flip):
    return [
        ((2 * a + b) * 2 + c, (2 * c + (b ^ flip)) * 2 + a)
        for a in range(2)
        for b in range(2)
        for c in range(2)
    ]


def weight_perm(zs, flip):
    return [
        (z * 8 + (2 * a + b) * 2 + c, z * 8 + (2 * c + (b ^ flip)) * 2 + (a ^ z % 2))
        for z in range(zs)
        for a in range(2)
        for b in range(2)
        for c in range(2)
    ]


def body(zs, tokens, weight, gain):
    shape = jax.ShapeDtypeStruct
    b = lax.rem(lax.axis_index("y"), 2)
    yc, zyc = ("y", "core"), ("z", "y", "core")
    core_swap = [(0, 1), (1, 0)]
    rows, mats = shape((512, HD), f32), lambda n: shape((n, HD, HD), f32)
    wide = shape((512, 3 * HD), f32)
    first, second = weight[:, :, :HD], weight[:, :, HD:]
    same = jnp.where(b == 0, first, second).transpose(1, 0, 2)
    flip = jnp.where(b == 0, second, first).transpose(1, 0, 2)
    same = lax.ppermute(same, zyc, weight_perm(zs, 0))
    flip = lax.ppermute(flip, zyc, weight_perm(zs, 1))
    part = shape((256, HD), bf16)
    keep, send = call(halve_kernel, (part, part), 10**5, 3 * 10**5)(tokens)
    got = lax.ppermute(send, "core", core_swap)
    tok = jnp.stack([keep, got])
    tok = jnp.broadcast_to(tok[None], (16,) + tok.shape)
    tok = lax.all_to_all(tok, ("x", "y"), 0, 0)
    own = lax.all_gather(
        jnp.stack([same, flip]), ("z", "core"), axis_index_groups=ring_groups(zs)
    )
    scratch = [pltpu.VMEM((zs * 64, 3 * HD), bf16)]
    send = call(functools.partial(project_kernel, False), wide, 400 * 10**6, 3 * 10**6, scratch)(tok, own)
    got = lax.ppermute(send, "core", core_swap)
    keep = call(functools.partial(project_kernel, True), wide, 400 * 10**6, 3 * 10**6, scratch)(tok, own)
    q, k, v, blk, pay = call(
        moment_kernel,
        (rows, rows, rows, mats(3), shape((4, ROWS, HD), f32)),
        600 * 10**6,
        3 * 10**6,
    )(keep, got)
    groups = [[(2 * p + i) * 2 + j for i in range(2) for j in range(2)] for p in range(zs // 2)]
    got = lax.all_to_all(pay, ("z", "core"), 0, 0, axis_index_groups=groups)
    gain, pay = lax.optimization_barrier((gain, pay))
    gain = gain.reshape(2, HD)
    gain_far = lax.ppermute(gain, "core", core_swap)
    raw = call(local_kernel, rows, 800 * 10**6, 2 * 10**6)(q, k, v, blk)
    total, inner, s_in = call(
        pair_kernel,
        (shape((PART, HD), f32), mats(2), shape((PACK, HD), f32)),
        10**8,
        10**6,
        [pltpu.VMEM((2 * PART, HD), f32)],
    )(got)
    totals = lax.all_gather(total, ("z", "core"), axis_index_groups=ring_groups(zs))
    totals = totals.reshape(zs // 2, 2 * PART, HD)
    s, keep, send = call(
        prior_kernel, (shape((HD, HD), f32), shape((HD, HALF), f32), shape((HD, HALF), f32)), 10**8, 10**6
    )(totals, inner, s_in)
    other_m = lax.ppermute(send, "core", core_swap)
    raw = call(cross_kernel, rows, 500 * 10**6, 2 * 10**6)(q, v, raw, blk, s)
    half = shape((256, HD), bf16)
    near, far = call(final_kernel, (half, half), 10**8, 10**6)(q, raw, keep, other_m, gain, gain_far)
    near = lax.ppermute(near, yc, pair_swap(0))
    far = lax.ppermute(far, yc, pair_swap(1))
    left = jnp.where(b == 0, near, far)
    right = jnp.where(b == 0, far, near)
    return jnp.concatenate([left, right], axis=1)


def solution(mesh):
    zs = mesh.shape["ctx"] // 4
    fine = Mesh(mesh.devices.reshape(zs, 4, 4, 2), ("z", "y", "x", "core"))
    ctx, head = ("z", "y"), ("x", "core")
    return jax.shard_map(
        functools.partial(body, zs),
        mesh=fine,
        in_specs=(P(ctx, head), P(ctx, None, head), P(head)),
        out_specs=P(ctx, head),
        check_vma=False,
    )
```

```python
import functools

import jax
import jax.numpy as jnp
from jax import lax
from jax.experimental import pallas as pl
from jax.experimental.pallas import tpu as pltpu
from jax.sharding import Mesh, PartitionSpec as P


HD = 128
HALF = HD // 2
PACK = 72
ROWS = PACK + HD
PART = 104
epsilon = 1e-06
f32 = jnp.float32
bf16 = jnp.bfloat16
VM = pl.BlockSpec(memory_space=pltpu.VMEM)


def split(x):
    high = x.astype(bf16)
    return high, (x - high.astype(f32)).astype(bf16)


def mm2(a, b, ca, cb):
    dims = (((ca,), (cb,)), ((), ()))
    dot = lambda x, y: lax.dot_general(x, y, dims, preferred_element_type=f32)
    return dot(a[0], b[0]) + (dot(a[0], b[1]) + dot(a[1], b[0]))


def mm(a, b, ca=1, cb=0):
    return mm2(split(a), split(b), ca, cb)


def dot(x, y, ca=1, cb=0):
    return lax.dot_general(x, y, (((ca,), (cb,)), ((), ())), preferred_element_type=f32)


def left3(x):
    return jnp.concatenate([x[0], x[0], x[1]], axis=1)


def right3(y, axis):
    return jnp.concatenate([y[0], y[1], y[0]], axis=axis)


def narrow(x, y, cy=0):
    return dot(left3(x), right3(y, cy), 1, cy)


def wide(x, y):
    both = dot(x[0], jnp.concatenate([y[0], y[1]], axis=1))
    return both[:, :HD] + both[:, HD:] + dot(x[1], y[0])


def tril(x):
    n = x.shape[0]
    rows = lax.broadcasted_iota(jnp.int32, (n, n), 0)
    cols = lax.broadcasted_iota(jnp.int32, (n, n), 1)
    return jnp.where(rows >= cols, x, 0.0)


def corner_ids():
    rows = lax.broadcasted_iota(jnp.int32, (HALF, HALF), 0)
    return rows, lax.broadcasted_iota(jnp.int32, (HALF, HALF), 1)


def triu(x):
    n = x.shape[0]
    rows = lax.broadcasted_iota(jnp.int32, (n, n), 0)
    cols = lax.broadcasted_iota(jnp.int32, (n, n), 1)
    return jnp.where(rows <= cols, x, 0.0)


def pack_sym(s):
    rows, cols = corner_ids()
    a, b, d = s[:HALF, :HALF], s[:HALF, HALF:], s[HALF:, HALF:]
    diag = jnp.sum(jnp.where(rows == cols, d, 0.0), axis=0, keepdims=True)
    diag = jnp.broadcast_to(jnp.concatenate([diag, diag], axis=1), (PACK - HALF, HD))
    return jnp.concatenate([jnp.concatenate([b, jnp.where(rows <= cols, a, d)], axis=1), diag], axis=0)


def unpack_sym(p):
    rows, cols = corner_ids()
    b, tri = p[:HALF, :HALF], p[:HALF, HALF:]
    flip = tri.T
    a = jnp.where(rows <= cols, tri, flip)
    d = jnp.where(rows > cols, tri, flip)
    d = jnp.where(rows == cols, p[HALF : HALF + 1, :HALF], d)
    return jnp.concatenate(
        [jnp.concatenate([a, b], axis=1), jnp.concatenate([b.T, d], axis=1)], axis=0
    )


def place():
    y = lax.axis_index("y")
    return lax.rem(y, 2), lax.axis_index("core")


def ring():
    return lax.rem(lax.axis_index("z") + lax.axis_index("core"), 2)


def ring_groups(zs):
    return [[z * 2 + (z + g) % 2 for z in range(zs)] for g in range(2)]


def halve_kernel(tok, keep_ref, send_ref):
    h = ring()
    left, right = tok[:, :HD], tok[:, HD:]
    even = jnp.concatenate([left[:, :HALF], right[:, :HALF]], axis=1)
    odd = jnp.concatenate([left[:, HALF:], right[:, HALF:]], axis=1)
    keep_ref[...] = jnp.where(h == 0, even, odd)
    send_ref[...] = jnp.where(h == 0, odd, even)


def project_kernel(mine, tok, own, out_ref, wf):
    b, c = place()
    half = c if mine else 1 - c
    for z in range(own.shape[0]):
        zh, z1, z0 = z // 4, z // 2 % 2, z % 2
        side = 128 * (c if z1 == 0 else 1 - c)
        for f in range(2):
            near = 32 * (b if f == 0 else 1 - b)
            at = pl.ds(pl.multiple_of(zh * 256 + 64 * z0 + side + near, 32), 32)
            for ch in range(3):
                wf[at, ch * HD : (ch + 1) * HD] = own[z, f, ch]
    for t in range(2):
        pieces = [(4 * f + 2 * half + t, side) for f in range(4) for side in range(2)]
        x = jnp.concatenate([tok[slot, side] for slot, side in pieces], axis=1)
        out_ref[256 * t : 256 * t + 256] = jnp.dot(x, wf[...], preferred_element_type=f32)


def moment_kernel(keep, got, q_ref, k_ref, v_ref, blk_ref, pay_ref, stage, sems):
    parts, sums = [], []
    for t in range(2):
        rows = slice(t * 256, t * 256 + 256)
        proj = keep[rows] + got[rows]
        q, k, v = proj[:, :HD], proj[:, HD : 2 * HD], proj[:, 2 * HD :]
        q_ref[rows], k_ref[rows], v_ref[rows] = q, k, v
        q2, k2, v2 = split(q), split(k), split(v)
        turned = (k2[0].T, k2[1].T)
        both = dot(turned[0], jnp.concatenate([k2[0], k2[1]], axis=1))
        s = both[:, :HD] + (both[:, HD:] + both[:, HD:].T)
        if t == 0:
            blk_ref[0] = s
        sums.append(s)
        parts.append((q2, k2, v2, turned))
    s_first = sums[0]
    packed = pack_sym(sums[0] + sums[1])
    stage[0, :PACK] = packed
    head = slice(0, PACK)
    copies = [
        pltpu.make_async_copy(stage.at[0, head], pay_ref.at[slot, head], sems.at[0, slot])
        for slot in range(4)
    ]
    for copy in copies:
        copy.start()
    for t, (q2, k2, v2, turned) in enumerate(parts):
        w2 = split(wide(split(triu(narrow(k2, q2, 1))), v2))
        m = wide(turned, w2)
        cc = wide((q2[0].T, q2[1].T), v2)
        if t == 0:
            c_all, m_all = cc, m
            blk_ref[1], blk_ref[2] = cc, m
        else:
            m_all = m_all + m + narrow(split(s_first), split(cc))
            c_all = c_all + cc
    tail = slice(PACK, ROWS)
    for h in range(2):
        cols = slice(h * HALF, h * HALF + HALF)
        stage[h, PACK:] = jnp.concatenate([c_all[:, cols], m_all[:, cols]], axis=1)
        for zb in range(2):
            slot = 2 * zb + (zb + h) % 2
            copy = pltpu.make_async_copy(stage.at[h, tail], pay_ref.at[slot, tail], sems.at[1, slot])
            copy.start()
            copies.append(copy)
    for copy in copies:
        copy.wait()


def local_kernel(q_ref, k_ref, v_ref, blk_ref, raw_ref):
    for t in range(2):
        rows = slice(t * 256, t * 256 + 256)
        q2 = split(q_ref[rows])
        low = split(tril(narrow(q2, split(k_ref[rows]), 1)))
        pair = mm2(low, low, 1, 1)
        if t == 1:
            qs = narrow(q2, split(blk_ref[0]))
            pair = pair + narrow(split(qs), q2, 1)
        raw = wide(split(tril(pair)), split(v_ref[rows]))
        if t == 1:
            raw = raw + narrow(q2, split(blk_ref[2]))
        raw_ref[rows] = raw


def pair_kernel(got, pay_ref, in_ref, s_in_ref, all_ref):
    _, c = place()
    zb = lax.rem(lax.axis_index("z"), 2)
    pos = 2 * zb + c
    s = jnp.zeros((PACK, HD), f32)
    cm = jnp.zeros((HD, HD), f32)
    s_in = s
    before = [cm, cm]
    left = lax.broadcasted_iota(jnp.int32, (HD, HD), 1) < HALF
    for i in range(4):
        s_in = jnp.where(pos == i, s, s_in)
        before[i % 2] = jnp.where(zb == i // 2, cm, before[i % 2])
        new = got[i, PACK:]
        if i:
            cross = mm(unpack_sym(s), new[:, :HALF])
            cross = jnp.concatenate([jnp.zeros_like(cross), cross], axis=1)
            cm = cm + new + cross
        else:
            cm = new
        s = s + got[i, :PACK]
    all_ref[:PACK] = s
    all_ref[PACK:ROWS] = cm
    all_ref[ROWS:] = jnp.zeros((2 * PART - ROWS, HD), f32)
    pay_ref[...] = all_ref[pl.ds(pl.multiple_of(zb * PART, 8), PART)]
    in_ref[0], in_ref[1] = before
    s_in_ref[...] = s_in


def prior_kernel(got, in_ref, s_in_ref, s_ref, keep_ref, send_ref):
    _, c = place()
    pair = lax.div(lax.axis_index("z"), 2)
    n = got.shape[0]
    s = jnp.zeros((PACK, HD), f32)
    m = jnp.zeros((HD, HALF), f32)
    lefts, rights = [], []
    for p in range(n - 1):
        live = p < pair
        if p:
            lefts.append(unpack_sym(s))
            rights.append(jnp.where(live, got[p, PACK:ROWS, :HALF], 0.0))
        m = m + jnp.where(live, got[p, PACK:ROWS, HALF:], 0.0)
        s = s + jnp.where(live, got[p, :PACK], 0.0)
    m = m + mm(jnp.concatenate(lefts, axis=1), jnp.concatenate(rights, axis=0))
    full = unpack_sym(s)
    both = jnp.concatenate([in_ref[0][:, :HALF], in_ref[1][:, :HALF]], axis=1)
    cross = mm(full, both)
    m0 = m + in_ref[0][:, HALF:] + cross[:, :HALF]
    m1 = m + in_ref[1][:, HALF:] + cross[:, HALF:]
    s_ref[...] = full + unpack_sym(s_in_ref[...])
    keep_ref[...] = jnp.where(c == 0, m0, m1)
    send_ref[...] = jnp.where(c == 0, m1, m0)


def cross_kernel(q_ref, v_ref, raw_ref, blk_ref, s_ref, out_ref):
    s2 = split(s_ref[...])
    for t in range(2):
        rows = slice(t * 256, t * 256 + 256)
        q2 = split(q_ref[rows])
        qs = split(narrow(q2, s2))
        scores = tril(narrow(qs, q2, 1))
        raw = raw_ref[rows] + wide(split(scores), split(v_ref[rows]))
        if t == 1:
            raw = raw + narrow(qs, split(blk_ref[1]))
        out_ref[rows] = raw


def final_kernel(q_ref, raw_ref, keep_ref, other_ref, gain_ref, gain_far_ref, near_ref, far_ref):
    b, c = place()
    h = ring()
    keep, other = keep_ref[...], other_ref[...]
    m2 = split(
        jnp.concatenate(
            [jnp.where(h == 0, keep, other), jnp.where(h == 0, other, keep)], axis=1
        )
    )
    y = lax.axis_index("y")
    gain = jnp.where(lax.div(y, 2) == c, gain_ref[...], gain_far_ref[...])
    gain = jnp.where(b == 0, gain[0:1], gain[1:2])
    for t in range(2):
        rows = slice(t * 256, t * 256 + 256)
        raw = raw_ref[rows] + narrow(split(q_ref[rows]), m2)
        mean_sq = jnp.mean(raw * raw, axis=-1, keepdims=True)
        out = (raw * lax.rsqrt(mean_sq + epsilon) * gain).astype(bf16)

        @pl.when(b == t)
        def _():
            near_ref[...] = out

        @pl.when(b != t)
        def _():
            far_ref[...] = out


def call(kernel, outs, flops, moved, scratch=(), **specs):
    return pl.pallas_call(
        kernel,
        **specs,
        out_shape=outs,
        scratch_shapes=list(scratch),
        compiler_params=pltpu.CompilerParams(vmem_limit_bytes=32 * 2**20),
        cost_estimate=pl.CostEstimate(flops=flops, bytes_accessed=moved, transcendentals=0),
    )


def pair_swap(flip):
    return [
        ((2 * a + b) * 2 + c, (2 * c + (b ^ flip)) * 2 + a)
        for a in range(2)
        for b in range(2)
        for c in range(2)
    ]


def weight_perm(zs, flip):
    return [
        (z * 8 + (2 * a + b) * 2 + c, z * 8 + (2 * c + (b ^ flip)) * 2 + (a ^ z % 2))
        for z in range(zs)
        for a in range(2)
        for b in range(2)
        for c in range(2)
    ]


def body(zs, tokens, weight, gain):
    shape = jax.ShapeDtypeStruct
    b = lax.rem(lax.axis_index("y"), 2)
    yc, zyc = ("y", "core"), ("z", "y", "core")
    core_swap = [(0, 1), (1, 0)]
    rows, mats = shape((512, HD), f32), lambda n: shape((n, HD, HD), f32)
    wide = shape((512, 3 * HD), f32)
    first, second = weight[:, :, :HD], weight[:, :, HD:]
    same = jnp.where(b == 0, first, second).transpose(1, 0, 2)
    flip = jnp.where(b == 0, second, first).transpose(1, 0, 2)
    same = lax.ppermute(same, zyc, weight_perm(zs, 0))
    flip = lax.ppermute(flip, zyc, weight_perm(zs, 1))
    part = shape((256, HD), bf16)
    keep, send = call(halve_kernel, (part, part), 10**5, 3 * 10**5)(tokens)
    got = lax.ppermute(send, "core", core_swap)
    tok = jnp.stack([keep, got])
    tok = jnp.broadcast_to(tok[None], (16,) + tok.shape)
    tok = lax.all_to_all(tok, ("x", "y"), 0, 0)
    own = lax.all_gather(
        jnp.stack([same, flip]), ("z", "core"), axis_index_groups=ring_groups(zs)
    )
    scratch = [pltpu.VMEM((zs * 64, 3 * HD), bf16)]
    send = call(functools.partial(project_kernel, False), wide, 400 * 10**6, 3 * 10**6, scratch)(tok, own)
    got = lax.ppermute(send, "core", core_swap)
    keep = call(functools.partial(project_kernel, True), wide, 400 * 10**6, 3 * 10**6, scratch)(tok, own)
    q, k, v, blk, pay = call(
        moment_kernel,
        (rows, rows, rows, mats(3), shape((4, ROWS, HD), f32)),
        600 * 10**6,
        3 * 10**6,
        [pltpu.VMEM((2, ROWS, HD), f32), pltpu.SemaphoreType.DMA((2, 4))],
        out_specs=(VM, VM, VM, VM, pl.BlockSpec(memory_space=pltpu.HBM)),
    )(keep, got)
    groups = [[(2 * p + i) * 2 + j for i in range(2) for j in range(2)] for p in range(zs // 2)]
    got = lax.all_to_all(pay, ("z", "core"), 0, 0, axis_index_groups=groups)
    gain, pay = lax.optimization_barrier((gain, pay))
    gain = gain.reshape(2, HD)
    gain_far = lax.ppermute(gain, "core", core_swap)
    raw = call(local_kernel, rows, 800 * 10**6, 2 * 10**6)(q, k, v, blk)
    total, inner, s_in = call(
        pair_kernel,
        (shape((PART, HD), f32), mats(2), shape((PACK, HD), f32)),
        10**8,
        10**6,
        [pltpu.VMEM((2 * PART, HD), f32)],
    )(got)
    totals = lax.all_gather(total, ("z", "core"), axis_index_groups=ring_groups(zs))
    totals = totals.reshape(zs // 2, 2 * PART, HD)
    s, keep, send = call(
        prior_kernel, (shape((HD, HD), f32), shape((HD, HALF), f32), shape((HD, HALF), f32)), 10**8, 10**6
    )(totals, inner, s_in)
    other_m = lax.ppermute(send, "core", core_swap)
    raw = call(cross_kernel, rows, 500 * 10**6, 2 * 10**6)(q, v, raw, blk, s)
    half = shape((256, HD), bf16)
    near, far = call(final_kernel, (half, half), 10**8, 10**6)(q, raw, keep, other_m, gain, gain_far)
    near = lax.ppermute(near, yc, pair_swap(0))
    far = lax.ppermute(far, yc, pair_swap(1))
    left = jnp.where(b == 0, near, far)
    right = jnp.where(b == 0, far, near)
    return jnp.concatenate([left, right], axis=1)


def solution(mesh):
    zs = mesh.shape["ctx"] // 4
    fine = Mesh(mesh.devices.reshape(zs, 4, 4, 2), ("z", "y", "x", "core"))
    ctx, head = ("z", "y"), ("x", "core")
    return jax.shard_map(
        functools.partial(body, zs),
        mesh=fine,
        in_specs=(P(ctx, head), P(ctx, None, head), P(head)),
        out_specs=P(ctx, head),
        check_vma=False,
    )
```

```python
import functools

import jax
import jax.numpy as jnp
from jax import lax
from jax.experimental import pallas as pl
from jax.experimental.pallas import tpu as pltpu
from jax.sharding import Mesh, PartitionSpec as P


HD = 128
HALF = HD // 2
PACK = 72
ROWS = PACK + HD
PART = 104
epsilon = 1e-06
f32 = jnp.float32
bf16 = jnp.bfloat16
VM = pl.BlockSpec(memory_space=pltpu.VMEM)


def split(x):
    high = x.astype(bf16)
    return high, (x - high.astype(f32)).astype(bf16)


def mm2(a, b, ca, cb):
    dims = (((ca,), (cb,)), ((), ()))
    dot = lambda x, y: lax.dot_general(x, y, dims, preferred_element_type=f32)
    return dot(a[0], b[0]) + (dot(a[0], b[1]) + dot(a[1], b[0]))


def mm(a, b, ca=1, cb=0):
    return mm2(split(a), split(b), ca, cb)


def dot(x, y, ca=1, cb=0):
    return lax.dot_general(x, y, (((ca,), (cb,)), ((), ())), preferred_element_type=f32)


def left3(x):
    return jnp.concatenate([x[0], x[0], x[1]], axis=1)


def right3(y, axis):
    return jnp.concatenate([y[0], y[1], y[0]], axis=axis)


def narrow(x, y, cy=0):
    return dot(left3(x), right3(y, cy), 1, cy)


def wide(x, y):
    both = dot(x[0], jnp.concatenate([y[0], y[1]], axis=1))
    return both[:, :HD] + both[:, HD:] + dot(x[1], y[0])


def tril(x):
    n = x.shape[0]
    rows = lax.broadcasted_iota(jnp.int32, (n, n), 0)
    cols = lax.broadcasted_iota(jnp.int32, (n, n), 1)
    return jnp.where(rows >= cols, x, 0.0)


def corner_ids():
    rows = lax.broadcasted_iota(jnp.int32, (HALF, HALF), 0)
    return rows, lax.broadcasted_iota(jnp.int32, (HALF, HALF), 1)


def triu(x):
    n = x.shape[0]
    rows = lax.broadcasted_iota(jnp.int32, (n, n), 0)
    cols = lax.broadcasted_iota(jnp.int32, (n, n), 1)
    return jnp.where(rows <= cols, x, 0.0)


def pack_sym(s):
    rows, cols = corner_ids()
    a, b, d = s[:HALF, :HALF], s[:HALF, HALF:], s[HALF:, HALF:]
    diag = jnp.sum(jnp.where(rows == cols, d, 0.0), axis=0, keepdims=True)
    diag = jnp.broadcast_to(jnp.concatenate([diag, diag], axis=1), (PACK - HALF, HD))
    return jnp.concatenate([jnp.concatenate([b, jnp.where(rows <= cols, a, d)], axis=1), diag], axis=0)


def unpack_sym(p):
    rows, cols = corner_ids()
    b, tri = p[:HALF, :HALF], p[:HALF, HALF:]
    flip = tri.T
    a = jnp.where(rows <= cols, tri, flip)
    d = jnp.where(rows > cols, tri, flip)
    d = jnp.where(rows == cols, p[HALF : HALF + 1, :HALF], d)
    return jnp.concatenate(
        [jnp.concatenate([a, b], axis=1), jnp.concatenate([b.T, d], axis=1)], axis=0
    )


def place():
    y = lax.axis_index("y")
    return lax.rem(y, 2), lax.axis_index("core")


def ring():
    return lax.rem(lax.axis_index("z") + lax.axis_index("core"), 2)


def ring_groups(zs):
    return [[z * 2 + (z + g) % 2 for z in range(zs)] for g in range(2)]


def halve_kernel(tok, keep_ref, send_ref):
    h = ring()
    left, right = tok[:, :HD], tok[:, HD:]
    even = jnp.concatenate([left[:, :HALF], right[:, :HALF]], axis=1)
    odd = jnp.concatenate([left[:, HALF:], right[:, HALF:]], axis=1)
    keep_ref[...] = jnp.where(h == 0, even, odd)
    send_ref[...] = jnp.where(h == 0, odd, even)


def project_kernel(mine, tok, own, out_ref, wf):
    b, c = place()
    half = c if mine else 1 - c
    for z in range(own.shape[0]):
        zh, z1, z0 = z // 4, z // 2 % 2, z % 2
        side = 128 * (c if z1 == 0 else 1 - c)
        for f in range(2):
            near = 32 * (b if f == 0 else 1 - b)
            at = pl.ds(pl.multiple_of(zh * 256 + 64 * z0 + side + near, 32), 32)
            for ch in range(3):
                wf[at, ch * HD : (ch + 1) * HD] = own[z, f, ch]
    for t in range(2):
        pieces = [(4 * f + 2 * half + t, side) for f in range(4) for side in range(2)]
        x = jnp.concatenate([tok[slot, side] for slot, side in pieces], axis=1)
        out_ref[256 * t : 256 * t + 256] = jnp.dot(x, wf[...], preferred_element_type=f32)


def moment_kernel(keep, got, q_ref, k_ref, v_ref, blk_ref, pay_ref):
    for t in range(2):
        rows = slice(t * 256, t * 256 + 256)
        proj = keep[rows] + got[rows]
        q, k, v = proj[:, :HD], proj[:, HD : 2 * HD], proj[:, 2 * HD :]
        q_ref[rows], k_ref[rows], v_ref[rows] = q, k, v
        q2, k2, v2 = split(q), split(k), split(v)
        w2 = split(wide(split(triu(narrow(k2, q2, 1))), v2))
        kh, kl = k2[0].T, k2[1].T
        a = dot(kh, jnp.concatenate([k2[0], k2[1], w2[0], w2[1]], axis=1))
        cross = a[:, HD : 2 * HD]
        s = a[:, :HD] + (cross + cross.T)
        m = a[:, 2 * HD : 3 * HD] + a[:, 3 * HD :] + dot(kl, w2[0])
        cc = wide((q2[0].T, q2[1].T), v2)
        if t == 0:
            s_all, c_all, m_all = s, cc, m
            blk_ref[0], blk_ref[1], blk_ref[2] = s, cc, m
        else:
            m_all = m_all + m + narrow(split(s_all), split(cc))
            s_all, c_all = s_all + s, c_all + cc
    packed = pack_sym(s_all)
    for h in range(2):
        cols = slice(h * HALF, h * HALF + HALF)
        half = jnp.concatenate([c_all[:, cols], m_all[:, cols]], axis=1)
        for zb in range(2):
            slot = 2 * zb + (zb + h) % 2
            pay_ref[slot, :PACK] = packed
            pay_ref[slot, PACK:] = half


def local_kernel(q_ref, k_ref, v_ref, blk_ref, raw_ref):
    for t in range(2):
        rows = slice(t * 256, t * 256 + 256)
        q2 = split(q_ref[rows])
        low = split(tril(narrow(q2, split(k_ref[rows]), 1)))
        pair = mm2(low, low, 1, 1)
        if t == 1:
            qs = narrow(q2, split(blk_ref[0]))
            pair = pair + narrow(split(qs), q2, 1)
        raw = wide(split(tril(pair)), split(v_ref[rows]))
        if t == 1:
            raw = raw + narrow(q2, split(blk_ref[2]))
        raw_ref[rows] = raw


def pair_kernel(got, pay_ref, in_ref, s_in_ref, all_ref):
    _, c = place()
    zb = lax.rem(lax.axis_index("z"), 2)
    pos = 2 * zb + c
    s = jnp.zeros((PACK, HD), f32)
    cm = jnp.zeros((HD, HD), f32)
    s_in = s
    before = [cm, cm]
    left = lax.broadcasted_iota(jnp.int32, (HD, HD), 1) < HALF
    for i in range(4):
        s_in = jnp.where(pos == i, s, s_in)
        before[i % 2] = jnp.where(zb == i // 2, cm, before[i % 2])
        new = got[i, PACK:]
        if i:
            cross = mm(unpack_sym(s), new[:, :HALF])
            cross = jnp.concatenate([jnp.zeros_like(cross), cross], axis=1)
            cm = cm + new + cross
        else:
            cm = new
        s = s + got[i, :PACK]
    all_ref[:PACK] = s
    all_ref[PACK:ROWS] = cm
    all_ref[ROWS:] = jnp.zeros((2 * PART - ROWS, HD), f32)
    pay_ref[...] = all_ref[pl.ds(pl.multiple_of(zb * PART, 8), PART)]
    in_ref[0], in_ref[1] = before
    s_in_ref[...] = s_in


def prior_kernel(got, in_ref, s_in_ref, s_ref, keep_ref, send_ref):
    _, c = place()
    pair = lax.div(lax.axis_index("z"), 2)
    n = got.shape[0]
    s = jnp.zeros((PACK, HD), f32)
    m = jnp.zeros((HD, HALF), f32)
    lefts, rights = [], []
    for p in range(n - 1):
        live = p < pair
        if p:
            lefts.append(unpack_sym(s))
            rights.append(jnp.where(live, got[p, PACK:ROWS, :HALF], 0.0))
        m = m + jnp.where(live, got[p, PACK:ROWS, HALF:], 0.0)
        s = s + jnp.where(live, got[p, :PACK], 0.0)
    m = m + mm(jnp.concatenate(lefts, axis=1), jnp.concatenate(rights, axis=0))
    full = unpack_sym(s)
    both = jnp.concatenate([in_ref[0][:, :HALF], in_ref[1][:, :HALF]], axis=1)
    cross = mm(full, both)
    m0 = m + in_ref[0][:, HALF:] + cross[:, :HALF]
    m1 = m + in_ref[1][:, HALF:] + cross[:, HALF:]
    s_ref[...] = full + unpack_sym(s_in_ref[...])
    keep_ref[...] = jnp.where(c == 0, m0, m1)
    send_ref[...] = jnp.where(c == 0, m1, m0)


def cross_kernel(q_ref, v_ref, raw_ref, blk_ref, s_ref, out_ref):
    s2 = split(s_ref[...])
    for t in range(2):
        rows = slice(t * 256, t * 256 + 256)
        q2 = split(q_ref[rows])
        qs = split(narrow(q2, s2))
        scores = tril(narrow(qs, q2, 1))
        raw = raw_ref[rows] + wide(split(scores), split(v_ref[rows]))
        if t == 1:
            raw = raw + narrow(qs, split(blk_ref[1]))
        out_ref[rows] = raw


def final_kernel(q_ref, raw_ref, keep_ref, other_ref, gain_ref, gain_far_ref, near_ref, far_ref):
    b, c = place()
    h = ring()
    keep, other = keep_ref[...], other_ref[...]
    m2 = split(
        jnp.concatenate(
            [jnp.where(h == 0, keep, other), jnp.where(h == 0, other, keep)], axis=1
        )
    )
    y = lax.axis_index("y")
    gain = jnp.where(lax.div(y, 2) == c, gain_ref[...], gain_far_ref[...])
    gain = jnp.where(b == 0, gain[0:1], gain[1:2])
    for t in range(2):
        rows = slice(t * 256, t * 256 + 256)
        raw = raw_ref[rows] + narrow(split(q_ref[rows]), m2)
        mean_sq = jnp.mean(raw * raw, axis=-1, keepdims=True)
        out = (raw * lax.rsqrt(mean_sq + epsilon) * gain).astype(bf16)

        @pl.when(b == t)
        def _():
            near_ref[...] = out

        @pl.when(b != t)
        def _():
            far_ref[...] = out


def call(kernel, outs, flops, moved, scratch=()):
    return pl.pallas_call(
        kernel,
        out_shape=outs,
        scratch_shapes=list(scratch),
        compiler_params=pltpu.CompilerParams(vmem_limit_bytes=32 * 2**20),
        cost_estimate=pl.CostEstimate(flops=flops, bytes_accessed=moved, transcendentals=0),
    )


def pair_swap(flip):
    return [
        ((2 * a + b) * 2 + c, (2 * c + (b ^ flip)) * 2 + a)
        for a in range(2)
        for b in range(2)
        for c in range(2)
    ]


def weight_perm(zs, flip):
    return [
        (z * 8 + (2 * a + b) * 2 + c, z * 8 + (2 * c + (b ^ flip)) * 2 + (a ^ z % 2))
        for z in range(zs)
        for a in range(2)
        for b in range(2)
        for c in range(2)
    ]


def body(zs, tokens, weight, gain):
    shape = jax.ShapeDtypeStruct
    b = lax.rem(lax.axis_index("y"), 2)
    yc, zyc = ("y", "core"), ("z", "y", "core")
    core_swap = [(0, 1), (1, 0)]
    rows, mats = shape((512, HD), f32), lambda n: shape((n, HD, HD), f32)
    wide = shape((512, 3 * HD), f32)
    first, second = weight[:, :, :HD], weight[:, :, HD:]
    same = jnp.where(b == 0, first, second).transpose(1, 0, 2)
    flip = jnp.where(b == 0, second, first).transpose(1, 0, 2)
    same = lax.ppermute(same, zyc, weight_perm(zs, 0))
    flip = lax.ppermute(flip, zyc, weight_perm(zs, 1))
    part = shape((256, HD), bf16)
    keep, send = call(halve_kernel, (part, part), 10**5, 3 * 10**5)(tokens)
    got = lax.ppermute(send, "core", core_swap)
    tok = jnp.stack([keep, got])
    tok = jnp.broadcast_to(tok[None], (16,) + tok.shape)
    tok = lax.all_to_all(tok, ("x", "y"), 0, 0)
    own = lax.all_gather(
        jnp.stack([same, flip]), ("z", "core"), axis_index_groups=ring_groups(zs)
    )
    scratch = [pltpu.VMEM((zs * 64, 3 * HD), bf16)]
    send = call(functools.partial(project_kernel, False), wide, 400 * 10**6, 3 * 10**6, scratch)(tok, own)
    got = lax.ppermute(send, "core", core_swap)
    keep = call(functools.partial(project_kernel, True), wide, 400 * 10**6, 3 * 10**6, scratch)(tok, own)
    q, k, v, blk, pay = call(
        moment_kernel,
        (rows, rows, rows, mats(3), shape((4, ROWS, HD), f32)),
        600 * 10**6,
        3 * 10**6,
    )(keep, got)
    groups = [[(2 * p + i) * 2 + j for i in range(2) for j in range(2)] for p in range(zs // 2)]
    got = lax.all_to_all(pay, ("z", "core"), 0, 0, axis_index_groups=groups)
    gain, pay = lax.optimization_barrier((gain, pay))
    gain = gain.reshape(2, HD)
    gain_far = lax.ppermute(gain, "core", core_swap)
    raw = call(local_kernel, rows, 800 * 10**6, 2 * 10**6)(q, k, v, blk)
    total, inner, s_in = call(
        pair_kernel,
        (shape((PART, HD), f32), mats(2), shape((PACK, HD), f32)),
        10**8,
        10**6,
        [pltpu.VMEM((2 * PART, HD), f32)],
    )(got)
    totals = lax.all_gather(total, ("z", "core"), axis_index_groups=ring_groups(zs))
    totals = totals.reshape(zs // 2, 2 * PART, HD)
    s, keep, send = call(
        prior_kernel, (shape((HD, HD), f32), shape((HD, HALF), f32), shape((HD, HALF), f32)), 10**8, 10**6
    )(totals, inner, s_in)
    other_m = lax.ppermute(send, "core", core_swap)
    raw = call(cross_kernel, rows, 500 * 10**6, 2 * 10**6)(q, v, raw, blk, s)
    half = shape((256, HD), bf16)
    near, far = call(final_kernel, (half, half), 10**8, 10**6)(q, raw, keep, other_m, gain, gain_far)
    near = lax.ppermute(near, yc, pair_swap(0))
    far = lax.ppermute(far, yc, pair_swap(1))
    left = jnp.where(b == 0, near, far)
    right = jnp.where(b == 0, far, near)
    return jnp.concatenate([left, right], axis=1)


def solution(mesh):
    zs = mesh.shape["ctx"] // 4
    fine = Mesh(mesh.devices.reshape(zs, 4, 4, 2), ("z", "y", "x", "core"))
    ctx, head = ("z", "y"), ("x", "core")
    return jax.shard_map(
        functools.partial(body, zs),
        mesh=fine,
        in_specs=(P(ctx, head), P(ctx, None, head), P(head)),
        out_specs=P(ctx, head),
        check_vma=False,
    )
```
